512 devices in a mesh: img: 8 (over y_lo, core), cin: 8 (over x, y_hi), cout: 8 (over z).
Axes of the slice: x: 4, y: 8 (y_hi: 2, y_lo: 4; y = y_hi * 4 + y_lo), z: 8, core: 2. Of those that a mesh axis runs over, the one named last changes fastest.
Arguments:
- maps: bfloat16 [2, 8, 14, 14, 1024], P(None, 'img'), may hold values from -6 to 6
- w_first: bfloat16 [3, 3, 1024, 1024], P(None, None, 'cin', 'cout'), may hold values from -0.09375 to 0.09375
- w_reduce: bfloat16 [3, 3, 1024, 8192], P(None, None, 'img', ('cin', 'cout')), may hold values from -0.09375 to 0.09375
- w_wide: bfloat16 [3, 3, 8192, 8192], P(None, None, 'cin', ('img', 'cout')), may hold values from -0.03125 to 0.03125
Outputs:
- wide_out: bfloat16 [2, 8, 7, 7, 8192], P(None, 'cin', None, None, ('img', 'cout'))
The draws below stay inside these ranges and needn't reach their ends.
All inputs are finite; a program needn't handle non-finite values.
Results may differ from the reference program's by a relative error of at most 0.014.
Values may be sent and summed in bfloat16 or wider, within the bound.
No kernel may reach another device: no remote copies, remote signals or barrier semaphores. Data moves between devices by JAX's collectives and lax.ppermute only.
A program may use at most 64 MiB of HBM per device.

```python
import jax
import jax.numpy as jnp

C1 = 1024
C2 = 8192
MAP = 14
MB = 2
HALF = 7
IMAGES = 8


def level_of(stream_key, shape, shards, least, top_value):
    def one(dim, shards_of):
        heights = jax.random.uniform(jax.random.fold_in(jax.random.fold_in(stream_key, 6), dim), (shards_of,), jnp.float32, least / len(shards), top_value / len(shards))
        return jnp.repeat(jnp.exp(heights), shape[dim] // shards_of).reshape((-1,) + (1,) * (len(shape) - dim - 1))

    level = one(*shards[0])
    for cut in shards[1:]:
        level = level * one(*cut)
    return level


def centred(own_key, dims, width, reach, split=(), kind=jnp.bfloat16):
    level = level_of(own_key, dims, split, -0.22, 0.18) if split else 1.0
    drawn = jax.random.normal(own_key, dims, jnp.float32) * width * level
    return jnp.minimum(jnp.maximum(drawn, -reach), reach).astype(kind)


def setup_inputs(seed: int = 0) -> dict:
    splits = jax.random.split(jax.random.key(seed), 5)
    return {
        "maps": centred(splits[0], (MB, IMAGES, MAP, MAP, C1), 1.0, 6.0, ((1, 8),)),
        "w_first": centred(splits[1], (3, 3, C1, C1), (9 * C1 // 2) ** -0.5, 0.09375, ((2, 8), (3, 8))),
        "w_reduce": centred(splits[2], (3, 3, C1, C2), (9 * C1 // 2) ** -0.5, 0.09375, ((2, 8), (3, 64))),
        "w_wide": centred(splits[3], (3, 3, C2, C2), (9 * C2 // 2) ** -0.5, 0.03125, ((2, 8), (3, 64))),
    }


def conv_taps(padded, weight, size, step):
    channels = padded.shape[3]
    windows = []
    for row_tap in range(3):
        for col_tap in range(3):
            windows.append(padded[:, row_tap:row_tap + step * (size - 1) + 1:step, col_tap:col_tap + step * (size - 1) + 1:step, :])
    table = jnp.concatenate(windows, axis=3).reshape(-1, 9 * channels)
    total = jnp.dot(table, weight.reshape(9 * channels, weight.shape[3]), preferred_element_type=jnp.float32)
    return total.reshape(padded.shape[0], size, size, weight.shape[3])


def pad_map(values):
    return jnp.pad(values, ((0, 0), (1, 1), (1, 1), (0, 0)))


def reference(maps, w_first, w_reduce, w_wide):
    flat = maps.reshape(MB * IMAGES, MAP, MAP, C1)
    rectified = jnp.maximum(flat, 0)
    segment_maps = (flat.astype(jnp.float32) + conv_taps(pad_map(rectified), w_first, MAP, 1)).astype(jnp.bfloat16)
    reduced = conv_taps(pad_map(jnp.maximum(segment_maps, 0)), w_reduce, HALF, 2)
    narrow = jnp.maximum(reduced, 0.0).astype(jnp.bfloat16)
    wide_out = conv_taps(pad_map(narrow), w_wide, HALF, 1).astype(jnp.bfloat16)
    return wide_out.reshape(MB, IMAGES, HALF, HALF, C2)
```

```python
import jax
import jax.numpy as jnp
from jax import lax
from jax.sharding import Mesh, PartitionSpec as P

YL, CORE, X, YH, Z = "yl", "core", "x", "yh", "z"
SIZES = (4, 2, 4, 2, 8)
IMG_Z_TURN = [(i * 8 + o, o * 8 + i) for i in range(8) for o in range(8)]
SWAP = [(0, 1), (1, 0)]
BF = jnp.bfloat16
F32 = jnp.float32


def exchange(values, axes):
    return lax.all_to_all(values, axes, 0, 0, tiled=True)


def both_cores(weight):
    other = lax.ppermute(weight, CORE, SWAP)
    first = lax.axis_index(CORE) == 0
    return jnp.concatenate([jnp.where(first, weight, other), jnp.where(first, other, weight)], axis=3)


def parity_planes(values):
    n, _, _, c = values.shape
    return values.reshape(n, 7, 2, 7, 2, c).transpose(2, 4, 0, 1, 3, 5).reshape(4, n, 7, 7, c)


def first_conv(part, weight):
    n, _, _, c = part.shape
    padded = jnp.pad(part, ((0, 0), (1, 1), (1, 1), (0, 0)))
    cells = padded.reshape(n, 8, 2, 8, 2, c).transpose(2, 4, 0, 1, 3, 5)
    cells = jnp.pad(cells, ((0, 0), (0, 0), (0, 0), (0, 0), (1, 0), (0, 0)))
    planes = []
    for row in range(2):
        for col in range(2):
            taps = []
            for a in range(3):
                for b in range(3):
                    i, qi = divmod(row + a, 2)
                    j, qj = divmod(col + b, 2)
                    taps.append(cells[qi, qj, :, i : i + 7, j : j + 8])
            planes.append(jnp.concatenate(taps, axis=3).reshape(n * 56, 9 * c))
    table = jnp.concatenate(planes, axis=0)
    return jnp.dot(table, weight.reshape(9 * c, -1), preferred_element_type=F32)


def reduce_conv(planes, weight):
    n, c = planes.shape[1], planes.shape[4]
    taps = []
    for a in range(3):
        for b in range(3):
            plane = planes[2 * ((a + 1) % 2) + (b + 1) % 2]
            if a == 0:
                plane = jnp.pad(plane[:, :6], ((0, 0), (1, 0), (0, 0), (0, 0)))
            if b == 0:
                plane = jnp.pad(plane[:, :, :7], ((0, 0), (0, 0), (1, 0), (0, 0)))
            taps.append(plane)
    table = jnp.concatenate(taps, axis=3).reshape(n * 56, 9 * c)
    return jnp.dot(table, weight.reshape(9 * c, -1), preferred_element_type=F32)


def wide_conv(maps, weight):
    n, groups, _, _, c = maps.shape
    padded = jnp.pad(maps, ((0, 0), (0, 0), (1, 1), (1, 1), (0, 0)))
    taps = []
    for a in range(3):
        for b in range(3):
            for g in range(groups):
                taps.append(padded[:, g, a : a + 7, b : b + 8])
    table = jnp.concatenate(taps, axis=3).reshape(n * 56, 9 * groups * c)
    return jnp.dot(table, weight.reshape(9 * groups * c, -1), preferred_element_type=F32)


def real_columns(values):
    column = lax.broadcasted_iota(jnp.int32, values.shape, values.ndim - 2)
    return jnp.where(column > 0, values, jnp.zeros_like(values))


def local(maps, w_first, w_reduce, w_wide):
    core = lax.axis_index(CORE)
    plane = lax.axis_index(X)
    in_block = lax.axis_index(X) * 2 + lax.axis_index(YH)
    out_block = lax.axis_index(Z)
    images = maps.reshape(2, 14, 14, 1024)
    part = lax.dynamic_slice_in_dim(images, in_block * 128, 128, 3)

    first = first_conv(jnp.maximum(part, 0), w_first).astype(BF).reshape(4, 1, 112, 128)
    first = exchange(jnp.broadcast_to(first, (4, 2, 112, 128)).reshape(8, 112, 128), (X, YH))
    summed = first.astype(F32).sum(0).reshape(2, 7, 8, 128)

    turned = lax.ppermute(w_reduce, (YL, CORE, Z), IMG_Z_TURN)
    weight_reduce = both_cores(turned)
    weight_wide = both_cores(w_wide)

    own = lax.dynamic_slice_in_dim(images, out_block * 128, 128, 3)
    own = lax.dynamic_index_in_dim(parity_planes(own), plane, 0, keepdims=False)
    own = jnp.pad(own, ((0, 0), (0, 0), (1, 0), (0, 0)))
    segment = (own.astype(F32) + summed).astype(BF)
    segment = real_columns(jnp.maximum(segment, 0)).reshape(2, 56, 128)

    send = jnp.broadcast_to(segment[None, :, None], (4, 2, 4, 56, 128)).reshape(32, 56, 128)
    planes = exchange(send, (YL, CORE, X)).reshape(8, 4, 7, 8, 128).transpose(1, 0, 2, 3, 4)

    reduced = reduce_conv(planes, weight_reduce).astype(BF).reshape(8, 56, 256)
    reduced = exchange(reduced, (Z,)).astype(F32).sum(0)
    narrow = real_columns(jnp.maximum(reduced, 0.0).astype(BF).reshape(7, 8, 256)).reshape(56, 256)

    gathered = exchange(jnp.broadcast_to(narrow, (32, 56, 256)), (YL, Z)).reshape(4, 8, 7, 8, 256)
    wide = wide_conv(gathered.transpose(1, 0, 2, 3, 4), weight_wide).astype(BF)

    wide = wide.reshape(8, 56, 2, 128).transpose(2, 0, 1, 3).reshape(16, 56, 128)
    wide = exchange(wide, (CORE, X, YH)).reshape(2, 8, 7, 8, 128)
    total = wide.astype(F32).sum(1).astype(BF)
    return total[:, None, :, 1:, :]


def solution(mesh):
    fine = Mesh(mesh.devices.reshape(SIZES), (YL, CORE, X, YH, Z))
    img, cin = (YL, CORE), (X, YH)
    in_specs = (
        P(None, img, None, None, None),
        P(None, None, cin, Z),
        P(None, None, img, cin + (Z,)),
        P(None, None, cin, img + (Z,)),
    )
    out_specs = P(None, cin, None, None, img + (Z,))
    return jax.shard_map(local, mesh=fine, in_specs=in_specs, out_specs=out_specs, check_vma=False)
```

```python
import jax
import jax.numpy as jnp
from jax import lax
from jax.experimental import pallas as pl
from jax.experimental.pallas import tpu as pltpu
from jax.sharding import Mesh, PartitionSpec as P


YL, CORE, X, YH, Z = "yl", "core", "x", "yh", "z"
SIZES = (4, 2, 4, 2, 8)
SWAP = [(0, 1), (1, 0)]
BF = jnp.bfloat16
F32 = jnp.float32


def exchange(values, axes):
    return lax.all_to_all(values, axes, 0, 0, tiled=True)


def swap_cores(values):
    return lax.ppermute(values, CORE, SWAP)


def parity_planes(values):
    n, _, _, c = values.shape
    return values.reshape(n, 7, 2, 7, 2, c).transpose(2, 4, 0, 1, 3, 5).reshape(4, n, 7, 7, c)


def first_conv(part, weight):
    n, _, _, c = part.shape
    padded = jnp.pad(part, ((0, 0), (1, 1), (1, 1), (0, 0)))
    cells = padded.reshape(n, 8, 2, 8, 2, c).transpose(2, 4, 0, 1, 3, 5)
    cells = jnp.pad(cells, ((0, 0), (0, 0), (0, 0), (0, 0), (1, 0), (0, 0)))
    planes = []
    for row in range(2):
        for col in range(2):
            taps = []
            for a in range(3):
                for b in range(3):
                    i, qi = divmod(row + a, 2)
                    j, qj = divmod(col + b, 2)
                    taps.append(cells[qi, qj, :, i : i + 7, j : j + 8])
            planes.append(jnp.concatenate(taps, axis=3).reshape(n * 56, 9 * c))
    table = jnp.concatenate(planes, axis=0)
    return jnp.dot(table, weight.reshape(9 * c, -1), preferred_element_type=F32)


def reduce_kernel(place, planes, mine, theirs, out):
    yl, core = place[0], place[1]
    row = lax.broadcasted_iota(jnp.int32, (112, 128), 0)
    inner = lax.rem(row // 8, 7) > 0
    total = jnp.zeros((112, 128), F32)
    for kind, weight in ((core, mine), (1 - core, theirs)):
        for shift in range(4):
            block = lax.rem(yl + (4 - shift), 4) * 2 + kind
            taps = {}
            for p in range(2):
                for q in range(2):
                    value = jnp.concatenate([planes[2 * p + q, n, block].astype(F32) for n in range(2)], axis=0)
                    for b in (0, 2) if q else (1,):
                        moved = pltpu.roll(value, 1, 0) if b == 0 else value
                        for a in (0, 2) if p else (1,):
                            tap = jnp.where(inner, pltpu.roll(moved, 8, 0), 0.0) if a == 0 else moved
                            taps[a, b] = tap.astype(BF)
            table = jnp.concatenate([taps[a, b] for a in range(3) for b in range(3)], axis=1)
            total = total + jnp.dot(table, weight[shift], preferred_element_type=F32)
    out[...] = jnp.where(lax.rem(row, 8) > 0, jnp.maximum(total, 0.0), 0.0).astype(BF)


def reduce_conv(place, planes, mine, theirs):
    vmem = pl.BlockSpec(memory_space=pltpu.VMEM)
    return pl.pallas_call(
        reduce_kernel,
        out_shape=jax.ShapeDtypeStruct((112, 128), BF),
        in_specs=[pl.BlockSpec(memory_space=pltpu.SMEM), vmem, vmem, vmem],
        out_specs=vmem,
        name="reduce_conv",
    )(place, planes, mine, theirs)


def wide_table(maps):
    n, groups, _, _, c = maps.shape
    padded = jnp.pad(maps, ((0, 0), (0, 0), (1, 1), (1, 1), (0, 0)))
    taps = []
    for a in range(3):
        for b in range(3):
            for g in range(groups):
                taps.append(padded[:, g, a : a + 7, b : b + 8])
    return jnp.concatenate(taps, axis=3).reshape(n * 56, 9 * groups * c)


def real_columns(values):
    column = lax.broadcasted_iota(jnp.int32, values.shape, values.ndim - 2)
    return jnp.where(column > 0, values, jnp.zeros_like(values))


def all_inputs(w_reduce):
    blocks = [w_reduce.reshape(1152, 128)]
    for shift in range(1, 4):
        blocks.append(lax.ppermute(blocks[0], YL, [(j, (j + shift) % 4) for j in range(4)]))
    mine = jnp.stack(blocks)
    theirs = swap_cores(mine)
    return mine, theirs


def body(maps, w_first, w_reduce, w_wide):
    core = lax.axis_index(CORE)
    plane = lax.axis_index(X)
    in_block = lax.axis_index(X) * 2 + lax.axis_index(YH)
    out_block = lax.axis_index(Z)
    images = maps.reshape(2, 14, 14, 1024)
    part = lax.dynamic_slice_in_dim(images, in_block * 128, 128, 3)

    first = first_conv(jnp.maximum(part, 0), w_first).astype(BF).reshape(4, 1, 112, 128)
    first = exchange(jnp.broadcast_to(first, (4, 2, 112, 128)).reshape(8, 112, 128), (X, YH))
    summed = first.astype(F32).sum(0).reshape(2, 7, 8, 128)

    mine, theirs = all_inputs(w_reduce)
    other = swap_cores(w_wide)
    weight_wide = jnp.concatenate(
        [jnp.where(core == 0, w_wide, other), jnp.where(core == 0, other, w_wide)], axis=3
    ).reshape(9216, 256)

    own = lax.dynamic_slice_in_dim(images, out_block * 128, 128, 3)
    own = lax.dynamic_index_in_dim(parity_planes(own), plane, 0, keepdims=False)
    own = jnp.pad(own, ((0, 0), (0, 0), (1, 0), (0, 0)))
    segment = (own.astype(F32) + summed).astype(BF)
    segment = real_columns(jnp.maximum(segment, 0)).reshape(2, 1, 56, 128)

    spread = jnp.broadcast_to(segment, (2, 8, 56, 128)).reshape(16, 56, 128)
    chip = exchange(spread, (CORE, Z)).reshape(896, 128)
    spread = jnp.broadcast_to(chip, (4, 896, 128))
    planes = exchange(spread, (X,)).reshape(4, 2, 8, 56, 128)
    place = jnp.stack([lax.axis_index(YL), core]).astype(jnp.int32)
    narrow = reduce_conv(place, planes, mine, theirs)

    gathered = exchange(jnp.broadcast_to(narrow, (32, 112, 128)), (YL, Z))
    gathered = gathered.reshape(4, 8, 2, 7, 8, 128).transpose(0, 2, 1, 3, 4, 5).reshape(8, 8, 7, 8, 128)
    wide = jnp.dot(wide_table(gathered), weight_wide, preferred_element_type=F32).astype(BF)

    wide = wide.reshape(8, 56, 256)
    wide = jnp.concatenate([wide[..., :128], wide[..., 128:]], axis=0)
    wide = exchange(wide, (CORE, X, YH)).reshape(2, 8, 7, 8, 128)
    total = wide.astype(F32).sum(1).astype(BF)
    return total[:, None, :, 1:, :]


def solution(mesh):
    fine = Mesh(mesh.devices.reshape(SIZES), (YL, CORE, X, YH, Z))
    img, cin = (YL, CORE), (X, YH)
    in_specs = (
        P(None, img, None, None, None),
        P(None, None, cin, Z),
        P(None, None, img, cin + (Z,)),
        P(None, None, cin, img + (Z,)),
    )
    out_specs = P(None, cin, None, None, img + (Z,))
    return jax.shard_map(body, mesh=fine, in_specs=in_specs, out_specs=out_specs, check_vma=False)
```

```python
import jax
import jax.numpy as jnp
from jax import lax
from jax.experimental import pallas as pl
from jax.experimental.pallas import tpu as pltpu
from jax.sharding import Mesh, PartitionSpec as P


YL, CORE, X, YH, Z = "yl", "core", "x", "yh", "z"
SIZES = (4, 2, 4, 2, 8)
SWAP = [(0, 1), (1, 0)]
BF = jnp.bfloat16
F32 = jnp.float32


def exchange(values, axes):
    return lax.all_to_all(values, axes, 0, 0, tiled=True)


def swap_cores(values):
    return lax.ppermute(values, CORE, SWAP)


def parity_planes(values):
    n, _, _, c = values.shape
    return values.reshape(n, 7, 2, 7, 2, c).transpose(2, 4, 0, 1, 3, 5).reshape(4, n, 7, 7, c)


def first_conv(part, weight):
    n, _, _, c = part.shape
    padded = jnp.pad(part, ((0, 0), (1, 1), (1, 1), (0, 0)))
    cells = padded.reshape(n, 8, 2, 8, 2, c).transpose(2, 4, 0, 1, 3, 5)
    cells = jnp.pad(cells, ((0, 0), (0, 0), (0, 0), (0, 0), (1, 0), (0, 0)))
    planes = []
    for row in range(2):
        for col in range(2):
            taps = []
            for a in range(3):
                for b in range(3):
                    i, qi = divmod(row + a, 2)
                    j, qj = divmod(col + b, 2)
                    taps.append(cells[qi, qj, :, i : i + 7, j : j + 8])
            planes.append(jnp.concatenate(taps, axis=3).reshape(n * 56, 9 * c))
    table = jnp.concatenate(planes, axis=0)
    return jnp.dot(table, weight.reshape(9 * c, -1), preferred_element_type=F32)


def nine_taps(value, rows, inner_top, inner_bottom):
    count = value.shape[0]
    taps = []
    for a in range(3):
        for b in range(3):
            moved = value if b == 1 else rows[b]
            if a == 0:
                moved = jnp.where(inner_top, pltpu.roll(moved, 8, 0), 0.0)
            elif a == 2:
                moved = jnp.where(inner_bottom, pltpu.roll(moved, count - 8, 0), 0.0)
            taps.append(moved.astype(BF))
    return jnp.concatenate(taps, axis=1)


def reduce_kernel(place, planes, mine, theirs, out, planes_v, mine_v, theirs_v, narrow, sems, out_sems):
    yl, core = place[0], place[1]
    copies = []
    for kind, source, held in ((0, mine, mine_v), (1, theirs, theirs_v)):
        own = core if kind == 0 else 1 - core
        for shift in range(4):
            step = 4 * kind + shift
            block = lax.rem(yl + (4 - shift), 4) * 2 + own
            pair = (
                pltpu.make_async_copy(planes.at[:, :, block], planes_v.at[step], sems.at[0, step]),
                pltpu.make_async_copy(source.at[shift], held.at[shift], sems.at[1, step]),
            )
            for copy in pair:
                copy.start()
            copies.append(pair)
    row = lax.broadcasted_iota(jnp.int32, (112, 128), 0)
    inner = lax.rem(row // 8, 7) > 0
    total = jnp.zeros((112, 128), F32)
    for step in range(8):
        for copy in copies[step]:
            copy.wait()
        taps = {}
        for p in range(2):
            for q in range(2):
                value = jnp.concatenate([planes_v[step, 2 * p + q, n].astype(F32) for n in range(2)], axis=0)
                for b in (0, 2) if q else (1,):
                    moved = pltpu.roll(value, 1, 0) if b == 0 else value
                    for a in (0, 2) if p else (1,):
                        tap = jnp.where(inner, pltpu.roll(moved, 8, 0), 0.0) if a == 0 else moved
                        taps[a, b] = tap.astype(BF)
        table = jnp.concatenate([taps[a, b] for a in range(3) for b in range(3)], axis=1)
        weight = (mine_v if step < 4 else theirs_v)[step % 4]
        total = total + jnp.dot(table, weight, preferred_element_type=F32)
    narrow[...] = jnp.where(lax.rem(row, 8) > 0, jnp.maximum(total, 0.0), 0.0).astype(BF)
    sent = [pltpu.make_async_copy(narrow, out.at[n], out_sems.at[n]) for n in range(32)]
    for copy in sent:
        copy.start()
    for copy in sent:
        copy.wait()


def reduce_conv(place, planes, mine, theirs):
    hbm = pl.BlockSpec(memory_space=pl.ANY)
    return pl.pallas_call(
        reduce_kernel,
        out_shape=jax.ShapeDtypeStruct((32, 112, 128), BF),
        in_specs=[pl.BlockSpec(memory_space=pltpu.SMEM), hbm, hbm, hbm],
        out_specs=hbm,
        scratch_shapes=[
            pltpu.VMEM((8, 4, 2, 56, 128), BF),
            pltpu.VMEM((4, 1152, 128), BF),
            pltpu.VMEM((4, 1152, 128), BF),
            pltpu.VMEM((112, 128), BF),
            pltpu.SemaphoreType.DMA((2, 8)),
            pltpu.SemaphoreType.DMA((32,)),
        ],
        name="reduce_conv",
    )(place, planes, mine, theirs)


def wide_kernel(place, maps, own, other, out, maps_v, own_v, other_v, sems):
    core = place[1]
    copies = []
    for z in range(8):
        channels = pl.ds(128 * z, 128)
        trio = (
            pltpu.make_async_copy(maps.at[:, z], maps_v.at[z], sems.at[0, z]),
            pltpu.make_async_copy(own.at[:, channels], own_v.at[z], sems.at[1, z]),
            pltpu.make_async_copy(other.at[:, channels], other_v.at[z], sems.at[2, z]),
        )
        for copy in trio:
            copy.start()
        copies.append(trio)
    line = lax.rem(lax.broadcasted_iota(jnp.int32, (448, 128), 0) // 8, 7)
    total = jnp.zeros((448, 256), F32)
    for z in range(8):
        for copy in copies[z]:
            copy.wait()
        value = maps_v[z].reshape(448, 128).astype(F32)
        rows = {0: pltpu.roll(value, 1, 0), 2: pltpu.roll(value, 447, 0)}
        table = nine_taps(value, rows, line > 0, line < 6)
        weight = jnp.concatenate([own_v[z].reshape(1152, 128), other_v[z].reshape(1152, 128)], axis=1)
        total = total + jnp.dot(table, weight, preferred_element_type=F32)
    out[core] = total[:, :128].astype(BF).reshape(8, 56, 128)
    out[1 - core] = total[:, 128:].astype(BF).reshape(8, 56, 128)


def wide_conv(place, maps, own, other):
    hbm = pl.BlockSpec(memory_space=pl.ANY)
    return pl.pallas_call(
        wide_kernel,
        out_shape=jax.ShapeDtypeStruct((2, 8, 56, 128), BF),
        in_specs=[pl.BlockSpec(memory_space=pltpu.SMEM), hbm, hbm, hbm],
        out_specs=pl.BlockSpec(memory_space=pltpu.VMEM),
        scratch_shapes=[
            pltpu.VMEM((8, 4, 112, 128), BF),
            pltpu.VMEM((8, 9, 128, 128), BF),
            pltpu.VMEM((8, 9, 128, 128), BF),
            pltpu.SemaphoreType.DMA((3, 8)),
        ],
        name="wide_conv",
    )(place, maps, own, other)


def real_columns(values):
    column = lax.broadcasted_iota(jnp.int32, values.shape, values.ndim - 2)
    return jnp.where(column > 0, values, jnp.zeros_like(values))


def all_inputs(w_reduce):
    blocks = [w_reduce.reshape(1152, 128)]
    for shift in range(1, 4):
        blocks.append(lax.ppermute(blocks[0], YL, [(j, (j + shift) % 4) for j in range(4)]))
    mine = jnp.stack(blocks)
    theirs = swap_cores(mine)
    return mine, theirs


def body(maps, w_first, w_reduce, w_wide):
    core = lax.axis_index(CORE)
    plane = lax.axis_index(X)
    in_block = lax.axis_index(X) * 2 + lax.axis_index(YH)
    out_block = lax.axis_index(Z)
    images = maps.reshape(2, 14, 14, 1024)
    part = lax.dynamic_slice_in_dim(images, in_block * 128, 128, 3)

    first = first_conv(jnp.maximum(part, 0), w_first).astype(BF).reshape(4, 1, 112, 128)
    first = exchange(jnp.broadcast_to(first, (4, 2, 112, 128)).reshape(8, 112, 128), (X, YH))
    summed = first.astype(F32).sum(0).reshape(2, 7, 8, 128)

    mine, theirs = all_inputs(w_reduce)
    other = swap_cores(w_wide)

    own = lax.dynamic_slice_in_dim(images, out_block * 128, 128, 3)
    own = lax.dynamic_index_in_dim(parity_planes(own), plane, 0, keepdims=False)
    own = jnp.pad(own, ((0, 0), (0, 0), (1, 0), (0, 0)))
    segment = (own.astype(F32) + summed).astype(BF)
    segment = real_columns(jnp.maximum(segment, 0)).reshape(2, 1, 56, 128)

    spread = jnp.broadcast_to(segment, (2, 8, 56, 128)).reshape(16, 56, 128)
    chip = exchange(spread, (CORE, Z)).reshape(896, 128)
    spread = jnp.broadcast_to(chip, (4, 896, 128))
    planes = exchange(spread, (X,)).reshape(4, 2, 8, 56, 128)
    place = jnp.stack([lax.axis_index(YL), core]).astype(jnp.int32)
    narrow = reduce_conv(place, planes, mine, theirs)

    gathered = exchange(narrow, (YL, Z)).reshape(4, 8, 112, 128)
    wide = wide_conv(place, gathered, w_wide.reshape(9, 1024, 128), other.reshape(9, 1024, 128))

    wide = wide.reshape(16, 56, 128)
    wide = exchange(wide, (CORE, X, YH)).reshape(2, 8, 7, 8, 128)
    total = wide.astype(F32).sum(1).astype(BF)
    return total[:, None, :, 1:, :]


def solution(mesh):
    fine = Mesh(mesh.devices.reshape(SIZES), (YL, CORE, X, YH, Z))
    img, cin = (YL, CORE), (X, YH)
    in_specs = (
        P(None, img, None, None, None),
        P(None, None, cin, Z),
        P(None, None, img, cin + (Z,)),
        P(None, None, cin, img + (Z,)),
    )
    out_specs = P(None, cin, None, None, img + (Z,))
    return jax.shard_map(body, mesh=fine, in_specs=in_specs, out_specs=out_specs, check_vma=False)
```

```python
import jax
import jax.numpy as jnp
from jax import lax
from jax.experimental import pallas as pl
from jax.experimental.pallas import tpu as pltpu
from jax.sharding import Mesh, PartitionSpec as P


YL, CORE, X, YH, Z = "yl", "core", "x", "yh", "z"
SIZES = (4, 2, 4, 2, 8)
SWAP = [(0, 1), (1, 0)]
BF = jnp.bfloat16
F32 = jnp.float32


def exchange(values, axes):
    return lax.all_to_all(values, axes, 0, 0, tiled=True)


def swap_cores(values):
    return lax.ppermute(values, CORE, SWAP)


def parity_planes(values):
    n, _, _, c = values.shape
    return values.reshape(n, 7, 2, 7, 2, c).transpose(2, 4, 0, 1, 3, 5).reshape(4, n, 7, 7, c)


def first_conv(part, weight):
    n, _, _, c = part.shape
    padded = jnp.pad(part, ((0, 0), (1, 1), (1, 1), (0, 0)))
    cells = padded.reshape(n, 8, 2, 8, 2, c).transpose(2, 4, 0, 1, 3, 5)
    cells = jnp.pad(cells, ((0, 0), (0, 0), (0, 0), (0, 0), (1, 0), (0, 0)))
    planes = []
    for row in range(2):
        for col in range(2):
            taps = []
            for a in range(3):
                for b in range(3):
                    i, qi = divmod(row + a, 2)
                    j, qj = divmod(col + b, 2)
                    taps.append(cells[qi, qj, :, i : i + 7, j : j + 8])
            planes.append(jnp.concatenate(taps, axis=3).reshape(n * 56, 9 * c))
    table = jnp.concatenate(planes, axis=0)
    return jnp.dot(table, weight.reshape(9 * c, -1), preferred_element_type=F32)


def reduce_kernel(place, planes, mine, theirs, out, planes_v, mine_v, theirs_v, narrow, sems, out_sems):
    yl, core = place[0], place[1]
    copies = []
    for kind, source, held in ((0, mine, mine_v), (1, theirs, theirs_v)):
        own = core if kind == 0 else 1 - core
        for shift in range(4):
            step = 4 * kind + shift
            block = lax.rem(yl + (4 - shift), 4) * 2 + own
            pair = (
                pltpu.make_async_copy(planes.at[:, :, block], planes_v.at[step], sems.at[0, step]),
                pltpu.make_async_copy(source.at[shift], held.at[shift], sems.at[1, step]),
            )
            for copy in pair:
                copy.start()
            copies.append(pair)
    row = lax.broadcasted_iota(jnp.int32, (112, 128), 0)
    inner = lax.rem(row // 8, 7) > 0
    total = jnp.zeros((112, 128), F32)
    for step in range(8):
        for copy in copies[step]:
            copy.wait()
        taps = {}
        for p in range(2):
            for q in range(2):
                value = jnp.concatenate([planes_v[step, 2 * p + q, n].astype(F32) for n in range(2)], axis=0)
                for b in (0, 2) if q else (1,):
                    moved = pltpu.roll(value, 1, 0) if b == 0 else value
                    for a in (0, 2) if p else (1,):
                        tap = jnp.where(inner, pltpu.roll(moved, 8, 0), 0.0) if a == 0 else moved
                        taps[a, b] = tap.astype(BF)
        table = jnp.concatenate([taps[a, b] for a in range(3) for b in range(3)], axis=1)
        weight = (mine_v if step < 4 else theirs_v)[step % 4]
        total = total + jnp.dot(table, weight, preferred_element_type=F32)
    narrow[...] = jnp.where(lax.rem(row, 8) > 0, jnp.maximum(total, 0.0), 0.0).astype(BF)
    sent = [pltpu.make_async_copy(narrow, out.at[n], out_sems.at[n]) for n in range(32)]
    for copy in sent:
        copy.start()
    for copy in sent:
        copy.wait()


def reduce_conv(place, planes, mine, theirs):
    hbm = pl.BlockSpec(memory_space=pl.ANY)
    return pl.pallas_call(
        reduce_kernel,
        out_shape=jax.ShapeDtypeStruct((32, 112, 128), BF),
        in_specs=[pl.BlockSpec(memory_space=pltpu.SMEM), hbm, hbm, hbm],
        out_specs=hbm,
        scratch_shapes=[
            pltpu.VMEM((8, 4, 2, 56, 128), BF),
            pltpu.VMEM((4, 1152, 128), BF),
            pltpu.VMEM((4, 1152, 128), BF),
            pltpu.VMEM((112, 128), BF),
            pltpu.SemaphoreType.DMA((2, 8)),
            pltpu.SemaphoreType.DMA((32,)),
        ],
        name="reduce_conv",
    )(place, planes, mine, theirs)


def wide_conv(maps, weight):
    n, _, _, c = maps.shape
    padded = jnp.pad(maps, ((0, 0), (1, 1), (1, 1), (0, 0)))
    table = jnp.concatenate([padded[:, a : a + 7, b : b + 8] for a in range(3) for b in range(3)], axis=3)
    return jnp.dot(table.reshape(n * 56, 9 * c), weight, preferred_element_type=F32)


def real_columns(values):
    column = lax.broadcasted_iota(jnp.int32, values.shape, values.ndim - 2)
    return jnp.where(column > 0, values, jnp.zeros_like(values))


def all_inputs(w_reduce):
    blocks = [w_reduce.reshape(1152, 128)]
    for shift in range(1, 4):
        blocks.append(lax.ppermute(blocks[0], YL, [(j, (j + shift) % 4) for j in range(4)]))
    mine = jnp.stack(blocks)
    theirs = swap_cores(mine)
    return mine, theirs


def body(maps, w_first, w_reduce, w_wide):
    core = lax.axis_index(CORE)
    plane = lax.axis_index(X)
    in_block = lax.axis_index(X) * 2 + lax.axis_index(YH)
    out_block = lax.axis_index(Z)
    images = maps.reshape(2, 14, 14, 1024)
    part = lax.dynamic_slice_in_dim(images, in_block * 128, 128, 3)

    first = first_conv(jnp.maximum(part, 0), w_first).astype(BF).reshape(4, 1, 112, 128)
    first = exchange(jnp.broadcast_to(first, (4, 2, 112, 128)).reshape(8, 112, 128), (X, YH))
    summed = first.astype(F32).sum(0).reshape(2, 7, 8, 128)

    mine, theirs = all_inputs(w_reduce)
    other = swap_cores(w_wide)
    weight_wide = jnp.concatenate(
        [jnp.where(core == 0, w_wide, other), jnp.where(core == 0, other, w_wide)], axis=3
    ).reshape(9216, 256)

    own = lax.dynamic_slice_in_dim(images, out_block * 128, 128, 3)
    own = lax.dynamic_index_in_dim(parity_planes(own), plane, 0, keepdims=False)
    own = jnp.pad(own, ((0, 0), (0, 0), (1, 0), (0, 0)))
    segment = (own.astype(F32) + summed).astype(BF)
    segment = real_columns(jnp.maximum(segment, 0)).reshape(2, 1, 56, 128)

    spread = jnp.broadcast_to(segment, (2, 8, 56, 128)).reshape(16, 56, 128)
    chip = exchange(spread, (CORE, Z)).reshape(896, 128)
    spread = jnp.broadcast_to(chip, (4, 896, 128))
    planes = exchange(spread, (X,)).reshape(4, 2, 8, 56, 128)
    place = jnp.stack([lax.axis_index(YL), core]).astype(jnp.int32)
    narrow = reduce_conv(place, planes, mine, theirs)

    gathered = exchange(narrow, (YL, Z)).reshape(4, 8, 2, 7, 8, 128)
    maps = jnp.concatenate([gathered[:, z] for z in range(8)], axis=4).reshape(8, 7, 8, 1024)
    wide = wide_conv(maps, weight_wide).astype(BF).reshape(8, 56, 256)

    wide = jnp.concatenate([wide[..., :128], wide[..., 128:]], axis=0)
    wide = exchange(wide, (CORE, X, YH)).reshape(2, 8, 7, 8, 128)
    total = wide.astype(F32).sum(1).astype(BF)
    return total[:, None, :, 1:, :]


def solution(mesh):
    fine = Mesh(mesh.devices.reshape(SIZES), (YL, CORE, X, YH, Z))
    img, cin = (YL, CORE), (X, YH)
    in_specs = (
        P(None, img, None, None, None),
        P(None, None, cin, Z),
        P(None, None, img, cin + (Z,)),
        P(None, None, cin, img + (Z,)),
    )
    out_specs = P(None, cin, None, None, img + (Z,))
    return jax.shard_map(body, mesh=fine, in_specs=in_specs, out_specs=out_specs, check_vma=False)
```

```python
import jax
import jax.numpy as jnp
from jax import lax
from jax.experimental import pallas as pl
from jax.experimental.pallas import tpu as pltpu
from jax.sharding import Mesh, PartitionSpec as P


YL, CORE, X, YH, Z = "yl", "core", "x", "yh", "z"
SIZES = (4, 2, 4, 2, 8)
SWAP = [(0, 1), (1, 0)]
BF = jnp.bfloat16
F32 = jnp.float32


def exchange(values, axes):
    return lax.all_to_all(values, axes, 0, 0, tiled=True)


def swap_cores(values):
    return lax.ppermute(values, CORE, SWAP)


def parity_planes(values):
    n, _, _, c = values.shape
    return values.reshape(n, 7, 2, 7, 2, c).transpose(2, 4, 0, 1, 3, 5).reshape(4, n, 7, 7, c)


def first_conv(part, weight):
    n, _, _, c = part.shape
    padded = jnp.pad(part, ((0, 0), (1, 1), (1, 1), (0, 0)))
    cells = padded.reshape(n, 8, 2, 8, 2, c).transpose(2, 4, 0, 1, 3, 5)
    cells = jnp.pad(cells, ((0, 0), (0, 0), (0, 0), (0, 0), (1, 0), (0, 0)))
    planes = []
    for row in range(2):
        for col in range(2):
            taps = []
            for a in range(3):
                for b in range(3):
                    i, qi = divmod(row + a, 2)
                    j, qj = divmod(col + b, 2)
                    taps.append(cells[qi, qj, :, i : i + 7, j : j + 8])
            planes.append(jnp.concatenate(taps, axis=3).reshape(n * 56, 9 * c))
    table = jnp.concatenate(planes, axis=0)
    return jnp.dot(table, weight.reshape(9 * c, -1), preferred_element_type=F32)


def reduce_kernel(place, planes, mine, theirs, out, planes_v, mine_v, theirs_v, narrow, sems, out_sems):
    yl, core = place[0], place[1]
    copies = []
    for kind, source, held in ((0, mine, mine_v), (1, theirs, theirs_v)):
        own = core if kind == 0 else 1 - core
        for shift in range(4):
            step = 4 * kind + shift
            block = lax.rem(yl + (4 - shift), 4) * 2 + own
            pair = (
                pltpu.make_async_copy(planes.at[:, :, block], planes_v.at[step], sems.at[0, step]),
                pltpu.make_async_copy(source.at[shift], held.at[shift], sems.at[1, step]),
            )
            for copy in pair:
                copy.start()
            copies.append(pair)
    row = lax.broadcasted_iota(jnp.int32, (112, 128), 0)
    inner = lax.rem(row // 8, 7) > 0
    total = jnp.zeros((112, 128), F32)
    for step in range(8):
        for copy in copies[step]:
            copy.wait()
        taps = {}
        for p in range(2):
            for q in range(2):
                value = jnp.concatenate([planes_v[step, 2 * p + q, n].astype(F32) for n in range(2)], axis=0)
                for b in (0, 2) if q else (1,):
                    moved = pltpu.roll(value, 1, 0) if b == 0 else value
                    for a in (0, 2) if p else (1,):
                        tap = jnp.where(inner, pltpu.roll(moved, 8, 0), 0.0) if a == 0 else moved
                        taps[a, b] = tap.astype(BF)
        table = jnp.concatenate([taps[a, b] for a in range(3) for b in range(3)], axis=1)
        weight = (mine_v if step < 4 else theirs_v)[step % 4]
        total = total + jnp.dot(table, weight, preferred_element_type=F32)
    narrow[...] = jnp.where(lax.rem(row, 8) > 0, jnp.maximum(total, 0.0), 0.0).astype(BF)
    sent = [pltpu.make_async_copy(narrow, out.at[n], out_sems.at[n]) for n in range(32)]
    for copy in sent:
        copy.start()
    for copy in sent:
        copy.wait()


def reduce_conv(place, planes, mine, theirs):
    hbm = pl.BlockSpec(memory_space=pl.ANY)
    return pl.pallas_call(
        reduce_kernel,
        out_shape=jax.ShapeDtypeStruct((32, 112, 128), BF),
        in_specs=[pl.BlockSpec(memory_space=pltpu.SMEM), hbm, hbm, hbm],
        out_specs=hbm,
        scratch_shapes=[
            pltpu.VMEM((8, 4, 2, 56, 128), BF),
            pltpu.VMEM((4, 1152, 128), BF),
            pltpu.VMEM((4, 1152, 128), BF),
            pltpu.VMEM((112, 128), BF),
            pltpu.SemaphoreType.DMA((2, 8)),
            pltpu.SemaphoreType.DMA((32,)),
        ],
        name="reduce_conv",
    )(place, planes, mine, theirs)


def wide_conv(maps, weight):
    n, _, _, c = maps.shape
    padded = jnp.pad(maps, ((0, 0), (1, 1), (1, 1), (0, 0)))
    table = jnp.concatenate([padded[:, a : a + 7, b : b + 8] for a in range(3) for b in range(3)], axis=3)
    return jnp.dot(table.reshape(n * 56, 9 * c), weight, preferred_element_type=F32)


def real_columns(values):
    column = lax.broadcasted_iota(jnp.int32, values.shape, values.ndim - 2)
    return jnp.where(column > 0, values, jnp.zeros_like(values))


def all_inputs(w_reduce):
    blocks = [w_reduce.reshape(1152, 128)]
    for shift in range(1, 4):
        blocks.append(lax.ppermute(blocks[0], YL, [(j, (j + shift) % 4) for j in range(4)]))
    mine = jnp.stack(blocks)
    theirs = swap_cores(mine)
    return mine, theirs


def body(maps, w_first, w_reduce, w_wide):
    core = lax.axis_index(CORE)
    plane = lax.axis_index(X)
    in_block = lax.axis_index(X) * 2 + lax.axis_index(YH)
    out_block = lax.axis_index(Z)
    images = maps.reshape(2, 14, 14, 1024)
    part = lax.dynamic_slice_in_dim(images, in_block * 128, 128, 3)

    first = first_conv(jnp.maximum(part, 0), w_first).astype(BF).reshape(4, 1, 112, 128)
    first = exchange(jnp.broadcast_to(first, (4, 2, 112, 128)).reshape(8, 112, 128), (X, YH))
    summed = first.astype(F32).sum(0).reshape(2, 7, 8, 128)

    mine, theirs = all_inputs(w_reduce)
    other = swap_cores(w_wide)
    weight_wide = jnp.concatenate([w_wide, other], axis=3).reshape(9216, 256)

    own = lax.dynamic_slice_in_dim(images, out_block * 128, 128, 3)
    own = lax.dynamic_index_in_dim(parity_planes(own), plane, 0, keepdims=False)
    own = jnp.pad(own, ((0, 0), (0, 0), (1, 0), (0, 0)))
    segment = (own.astype(F32) + summed).astype(BF)
    segment = real_columns(jnp.maximum(segment, 0)).reshape(2, 1, 56, 128)

    spread = jnp.broadcast_to(segment, (2, 8, 56, 128)).reshape(16, 56, 128)
    chip = exchange(spread, (CORE, Z)).reshape(896, 128)
    spread = jnp.broadcast_to(chip, (4, 896, 128))
    planes = exchange(spread, (X,)).reshape(4, 2, 8, 56, 128)
    place = jnp.stack([lax.axis_index(YL), core]).astype(jnp.int32)
    narrow = reduce_conv(place, planes, mine, theirs)

    gathered = exchange(narrow, (YL, Z)).reshape(4, 8, 2, 7, 8, 128)
    maps = jnp.concatenate([gathered[:, z] for z in range(8)], axis=4).reshape(8, 7, 8, 1024)
    wide = wide_conv(maps, weight_wide).astype(BF).reshape(8, 56, 256)

    mine, other = wide[..., :128], wide[..., 128:]
    wide = jnp.concatenate([jnp.where(core == 0, mine, other), jnp.where(core == 0, other, mine)], axis=0)
    wide = exchange(wide, (CORE, X, YH)).reshape(2, 8, 7, 8, 128)
    total = wide.astype(F32).sum(1).astype(BF)
    return total[:, None, :, 1:, :]


def solution(mesh):
    fine = Mesh(mesh.devices.reshape(SIZES), (YL, CORE, X, YH, Z))
    img, cin = (YL, CORE), (X, YH)
    in_specs = (
        P(None, img, None, None, None),
        P(None, None, cin, Z),
        P(None, None, img, cin + (Z,)),
        P(None, None, cin, img + (Z,)),
    )
    out_specs = P(None, cin, None, None, img + (Z,))
    return jax.shard_map(body, mesh=fine, in_specs=in_specs, out_specs=out_specs, check_vma=False)
```
